256 devices in a mesh: panel: 64 (over y, z, core), chan: 4 (over x).
Axes of the slice: x: 4, y: 4, z: 8, core: 2. Of those that a mesh axis runs over, the one named last changes fastest.
Arguments:
- wavefunction: bfloat16 [4, 64, 768, 768], P('chan', 'panel'), may hold values from -6 to 6
- left_env: bfloat16 [2, 64, 768, 768], P(None, 'panel'), may hold values from -0.21875 to 0.21875
- right_env: bfloat16 [2, 64, 768, 768], P(None, 'panel'), may hold values from -0.21875 to 0.21875
- coupling: float32 [2, 4, 4], replicated, may hold values from -4 to 4
- sec_size: int32 [64], replicated, may hold values from 384 to 768, as said below
Outputs:
- applied: bfloat16 [4, 64, 768, 768], P('chan', 'panel')
The draws below stay inside these ranges and needn't reach their ends.
Inputs may be any that keep to these rules, and one draw needn't show every extreme that they name: `sec_size`: sector sizes; some sector holds exactly 768 states.
All inputs are finite; a program needn't handle non-finite values.
Results may differ from the reference program's by a relative error of at most 0.008.
Values may be sent and summed in bfloat16 or wider, within the bound.
No kernel may reach another device: no remote copies, remote signals or barrier semaphores. Data moves between devices by JAX's collectives and lax.ppermute only.
A program may use at most 128 MiB of HBM per device.

```python
import jax
import jax.numpy as jnp
from jax import lax

M = 768
PAIRS = 4
CHANNELS = 2
NSEC = 64


def draw_sec_size(key, part):
    values = jax.random.randint(jax.random.fold_in(key, 11), (NSEC,), M // 2, M + 1, dtype=jnp.int32)
    chosen = jax.random.randint(jax.random.fold_in(key, 12), (), 0, NSEC, dtype=jnp.int32)
    slot_ids = jnp.arange(NSEC, dtype=jnp.int32)
    return jnp.where(slot_ids == chosen, M, values).astype(jnp.int32)


def block_scale(key, shape, shards, smallest, largest):
    factor_of = 1.0
    for axis_at, parts in shards:
        heights = jax.random.uniform(jax.random.fold_in(jax.random.fold_in(key, 6), axis_at), (parts,), jnp.float32, smallest / len(shards), largest / len(shards))
        factor_of = factor_of * jnp.repeat(jnp.exp(heights), shape[axis_at] // parts).reshape((-1,) + (1,) * (len(shape) - 1 - axis_at))
    return factor_of


def normal_values(stream_key, extent, scale, bound, shards=(), held_as=jnp.bfloat16):
    values = jax.random.normal(stream_key, extent, jnp.float32) * scale
    if len(shards) > 0:
        values = block_scale(stream_key, extent, shards, -0.22, 0.18) * values
    return jnp.clip(values, min=-bound, max=bound).astype(held_as)


def setup_inputs(seed: int = 0) -> dict:
    streams_of = jax.random.split(jax.random.key(seed), 6)
    wavefunction = normal_values(streams_of[0], (PAIRS, NSEC, M, M), 1.0, 6.0, ((0, 4), (1, 64)))
    left_env = normal_values(streams_of[1], (CHANNELS, NSEC, M, M), M ** -0.5, 0.21875, ((1, 64),))
    right_env = normal_values(streams_of[2], (CHANNELS, NSEC, M, M), M ** -0.5, 0.21875, ((1, 64),))
    coupling = normal_values(streams_of[3], (CHANNELS, PAIRS, PAIRS), 1.0, 4.0, (), jnp.float32)
    sec_size = draw_sec_size(jax.random.fold_in(streams_of[5], 71), 0)
    return {"wavefunction": wavefunction, "left_env": left_env, "right_env": right_env, "coupling": coupling, "sec_size": sec_size}


CHARGE_TABLE = (0, 1, 1, 2)


def outer_dot(left_matrix, right_matrix):
    return lax.dot_general(left_matrix, right_matrix, (((1,), (1,)), ((), ())), preferred_element_type=jnp.float32)


def coupling_masks(coupling):
    charges = jnp.array(CHARGE_TABLE, jnp.int32)
    same_charge = charges[:, None] == charges[None, :]
    raised_charge = charges[None, :] == charges[:, None] + 1
    return jnp.where(same_charge, coupling[0], 0.0), jnp.where(raised_charge, coupling[1], 0.0)


def reference(wavefunction, left_env, right_env, coupling, sec_size):
    same_coef, raise_coef = coupling_masks(coupling)
    positions = jnp.arange(M, dtype=jnp.int32)

    def block_mask(sector, charge_value):
        target = sector + charge_value
        exists = jnp.logical_and(target < NSEC, sector >= 0)
        rows_live = sec_size[jnp.clip(sector, 0, NSEC - 1)]
        cols_live = sec_size[jnp.clip(target, 0, NSEC - 1)]
        row_ok = positions[:, None] < rows_live
        col_ok = positions[None, :] < cols_live
        return jnp.logical_and(jnp.logical_and(row_ok, col_ok), exists)

    def right_block(channel, target):
        clipped = jnp.clip(target, 0, NSEC - 1).astype(jnp.int32)
        found = right_env[channel, clipped]
        inside = jnp.logical_and(target >= 0, target < NSEC)
        return jnp.where(inside, found, jnp.zeros_like(found))

    def one_sector(sector):
        previous = jnp.maximum(sector - 1, 0)
        summed = jnp.zeros((PAIRS, M, M), jnp.float32)
        for source in range(PAIRS):
            charge_value = CHARGE_TABLE[source]
            here_block = wavefunction[source, sector]
            here = jnp.where(block_mask(sector, charge_value), here_block, jnp.zeros_like(here_block))
            lower_block = wavefunction[source, previous]
            lower_ok = jnp.logical_and(block_mask(sector - 1, charge_value), sector >= 1)
            lower = jnp.where(lower_ok, lower_block, jnp.zeros_like(lower_block))
            same_sector = jnp.dot(left_env[0, sector], here, preferred_element_type=jnp.float32).astype(jnp.bfloat16)
            raised = jnp.dot(left_env[1, sector], lower, preferred_element_type=jnp.float32).astype(jnp.bfloat16)
            kept_terms = outer_dot(same_sector, right_block(0, sector + charge_value))
            moved_terms = outer_dot(raised, right_block(1, sector - 1 + charge_value))
            summed = summed + same_coef[:, source][:, None, None] * kept_terms[None] + raise_coef[:, source][:, None, None] * moved_terms[None]
        masks = jnp.stack([block_mask(sector, CHARGE_TABLE[target_pair]) for target_pair in range(PAIRS)])
        return jnp.where(masks, summed, 0.0).astype(jnp.bfloat16)

    result = lax.map(one_sector, jnp.arange(NSEC, dtype=jnp.int32))
    return jnp.transpose(result, (1, 0, 2, 3))
```

```python
import jax
import jax.numpy as jnp
from jax import lax
from jax.experimental import pallas as pl
from jax.experimental.pallas import tpu as pltpu
from jax.sharding import PartitionSpec as P

CHUNKS = 2
TILE = 256
AXES = ("panel", "chan")


def move(block, sectors, routes):
    pairs = lax.axis_size("chan")
    hops = []
    for source, target, shift in routes:
        for a in range(sectors):
            if 0 <= a + shift < sectors:
                hops.append((a * pairs + source, (a + shift) * pairs + target))
    return lax.ppermute(block, AXES, hops)


def outer_dot(left_matrix, right_matrix):
    return lax.dot_general(
        left_matrix, right_matrix, (((1,), (1,)), ((), ())), preferred_element_type=jnp.float32
    )


def live(sizes, sector):
    count = sizes.shape[0]
    inside = jnp.logical_and(sector >= 0, sector < count)
    return jnp.where(inside, sizes[jnp.clip(sector, 0, count - 1)], 0)


def charge_of(pair):
    return jnp.where(pair == 0, 0, jnp.where(pair == 3, 2, 1))


def inside(rows, cols, first_row, shape):
    row = first_row + lax.broadcasted_iota(jnp.int32, shape, 0)
    col = lax.broadcasted_iota(jnp.int32, shape, 1)
    return jnp.logical_and(row < rows, col < cols)


def kept_kernel(coupling, sizes, *refs):
    own_ref, *rest = refs
    partner = rest[:CHUNKS]
    left_ref, right_ref, near_ref, far_ref, acc_ref, left, own, other, right, sems = rest[CHUNKS:]
    width = own.shape[0]
    step = width // CHUNKS
    pair = lax.axis_index("chan")
    sector = lax.axis_index("panel")
    middle = jnp.logical_or(pair == 1, pair == 2)
    pltpu.make_async_copy(left_ref.at[0, 0], left, sems.at[0]).start()
    pltpu.make_async_copy(own_ref.at[0, 0], own, sems.at[1]).start()

    @pl.when(pair == 0)
    def _():
        pltpu.make_async_copy(right_ref.at[0, 0], right, sems.at[2]).start()

    @pl.when(middle)
    def _():
        pltpu.make_async_copy(near_ref.at[0, 0], right, sems.at[2]).start()

    @pl.when(pair == 3)
    def _():
        pltpu.make_async_copy(far_ref, right, sems.at[2]).start()

    for i in range(CHUNKS):
        pltpu.make_async_copy(partner[i], other.at[pl.ds(i * step, step)], sems.at[3 + i]).start()
    alpha = coupling[0, pair, pair]
    beta = jnp.where(middle, coupling[0, pair, jnp.where(middle, 3 - pair, 0)], 0.0)
    rows = live(sizes, sector)
    cols = live(sizes, sector + charge_of(pair))
    pltpu.make_async_copy(own_ref.at[0, 0], own, sems.at[1]).wait()
    for i in range(CHUNKS):
        pltpu.make_async_copy(partner[i], other.at[pl.ds(i * step, step)], sems.at[3 + i]).wait()
    for at in range(0, width, TILE):
        window = pl.ds(at, TILE)
        mixed = alpha * own[window].astype(jnp.float32)
        mixed = jnp.where(middle, mixed + beta * other[window].astype(jnp.float32), mixed)
        keep = inside(rows, cols, at, mixed.shape)
        own[window] = jnp.where(keep, mixed, 0.0).astype(jnp.bfloat16)
    pltpu.make_async_copy(left_ref.at[0, 0], left, sems.at[0]).wait()
    pltpu.make_async_copy(right_ref.at[0, 0], right, sems.at[2]).wait()
    for at in range(0, width, TILE):
        window = pl.ds(at, TILE)
        half = jnp.dot(left[window], own[...], preferred_element_type=jnp.float32)
        acc_ref[window] = outer_dot(half.astype(jnp.bfloat16), right[...])


def moved_kernel(coupling, sizes, *refs):
    acc_ref, *rest = refs
    relayed = rest[:CHUNKS]
    direct_ref, left_ref, right_ref, near_ref, out_ref, left, lower, right, sems = rest[CHUNKS:]
    width = lower.shape[0]
    step = width // CHUNKS
    pair = lax.axis_index("chan")
    sector = lax.axis_index("panel")
    rows = live(sizes, sector)
    cols = live(sizes, sector + charge_of(pair))

    @pl.when(pair == 3)
    def _():
        for at in range(0, width, TILE):
            window = pl.ds(at, TILE)
            keep = inside(rows, cols, at, (TILE, width))
            out_ref[0, 0, window] = jnp.where(keep, acc_ref[window], 0.0).astype(jnp.bfloat16)

    @pl.when(pair != 3)
    def _():
        pltpu.make_async_copy(left_ref.at[1, 0], left, sems.at[0]).start()

        @pl.when(pair == 0)
        def _():
            pltpu.make_async_copy(right_ref.at[1, 0], right, sems.at[1]).start()

        @pl.when(pair != 0)
        def _():
            pltpu.make_async_copy(near_ref.at[1, 0], right, sems.at[1]).start()

        @pl.when(pair == 2)
        def _():
            copy = pltpu.make_async_copy(direct_ref.at[0, 0], lower, sems.at[2])
            copy.start()
            copy.wait()

        @pl.when(pair != 2)
        def _():
            copies = [
                pltpu.make_async_copy(relayed[i], lower.at[pl.ds(i * step, step)], sems.at[2 + i])
                for i in range(CHUNKS)
            ]
            for copy in copies:
                copy.start()
            for copy in copies:
                copy.wait()

        lower_rows = live(sizes, sector - 1)
        gamma = jnp.where(pair == 0, 1.0, coupling[1, pair, 3])
        for at in range(0, width, TILE):
            window = pl.ds(at, TILE)
            keep = inside(lower_rows, cols, at, (TILE, width))
            lower[window] = jnp.where(keep, lower[window].astype(jnp.float32), 0.0).astype(jnp.bfloat16)
        pltpu.make_async_copy(left_ref.at[1, 0], left, sems.at[0]).wait()
        pltpu.make_async_copy(right_ref.at[1, 0], right, sems.at[1]).wait()
        for at in range(0, width, TILE):
            window = pl.ds(at, TILE)
            half = jnp.dot(left[window], lower[...], preferred_element_type=jnp.float32)
            term = outer_dot((gamma * half).astype(jnp.bfloat16), right[...])
            keep = inside(rows, cols, at, term.shape)
            out_ref[0, 0, window] = jnp.where(keep, acc_ref[window] + term, 0.0).astype(jnp.bfloat16)


def shards(wavefunction, left_env, right_env, coupling, sec_size):
    width = wavefunction.shape[-1]
    sectors = sec_size.shape[0]
    step = width // CHUNKS
    own = wavefunction[0, 0]
    pair = lax.axis_index("chan")
    own_part = [own[i * step : (i + 1) * step] for i in range(CHUNKS)]
    partner = [move(part, sectors, ((1, 2, 0), (2, 1, 0), (3, 0, 0))) for part in own_part]
    near = move(right_env, sectors, ((1, 1, -1), (2, 2, -1)))
    direct = move(wavefunction, sectors, ((3, 2, 1),))
    far = move(right_env[0, 0], sectors, ((3, 3, -2),))
    mine = jnp.where(pair == 1, coupling[1, 0, 1], 0.0)
    theirs = jnp.where(pair == 1, coupling[1, 0, 2], 1.0)
    onward = []
    for a, b in zip(own_part, partner):
        if onward:
            b, onward[-1] = lax.optimization_barrier((b, onward[-1]))
        mixed = mine * a.astype(jnp.float32) + theirs * b.astype(jnp.float32)
        onward.append(mixed.astype(jnp.bfloat16))
    relayed = [move(part, sectors, ((1, 0, 1), (0, 1, 1))) for part in onward]

    anywhere = pl.BlockSpec(memory_space=pl.ANY)
    scalars = pl.BlockSpec(memory_space=pltpu.SMEM)
    block = pltpu.VMEM((width, width), jnp.bfloat16)
    flops = 2 * 2 * width**3
    acc = pl.pallas_call(
        kept_kernel,
        out_shape=jax.ShapeDtypeStruct((width, width), jnp.float32),
        in_specs=[scalars] * 2 + [anywhere] * (5 + CHUNKS),
        out_specs=pl.BlockSpec(memory_space=pltpu.VMEM),
        scratch_shapes=[block, block, block, block, pltpu.SemaphoreType.DMA((3 + CHUNKS,))],
        cost_estimate=pl.CostEstimate(flops=flops, bytes_accessed=12 * width * width, transcendentals=0),
        name="kept",
    )(coupling, sec_size, wavefunction, *partner, left_env, right_env, near, far)
    out = pl.pallas_call(
        moved_kernel,
        out_shape=jax.ShapeDtypeStruct((1, 1, width, width), jnp.bfloat16),
        in_specs=[scalars] * 2
        + [pl.BlockSpec(memory_space=pltpu.VMEM)]
        + [anywhere] * (4 + CHUNKS),
        out_specs=pl.BlockSpec(memory_space=pltpu.VMEM),
        scratch_shapes=[block, block, block, pltpu.SemaphoreType.DMA((2 + CHUNKS,))],
        cost_estimate=pl.CostEstimate(flops=flops, bytes_accessed=12 * width * width, transcendentals=0),
        name="moved",
    )(coupling, sec_size, acc, *relayed, direct, left_env, right_env, near)
    return out


def solution(mesh):
    return jax.shard_map(
        shards,
        mesh=mesh,
        in_specs=(
            P("chan", "panel", None, None),
            P(None, "panel", None, None),
            P(None, "panel", None, None),
            P(),
            P(),
        ),
        out_specs=P("chan", "panel", None, None),
        check_vma=False,
    )
```

```python
import jax
import jax.numpy as jnp
from jax import lax
from jax.experimental import pallas as pl
from jax.experimental.pallas import tpu as pltpu
from jax.sharding import PartitionSpec as P


WIDTHS = (256, 256, 256)
STARTS = tuple(sum(WIDTHS[:i]) for i in range(len(WIDTHS)))
LATE = 1
TILE = 256
AXES = ("panel", "chan")
VMEM_BYTES = 24 * 1024 * 1024


def move(block, sectors, routes):
    pairs = lax.axis_size("chan")
    hops = []
    for source, target, shift in routes:
        for a in range(sectors):
            if 0 <= a + shift < sectors:
                hops.append((a * pairs + source, (a + shift) * pairs + target))
    return lax.ppermute(block, AXES, hops)


def outer_dot(left_matrix, right_matrix):
    return lax.dot_general(
        left_matrix, right_matrix, (((1,), (1,)), ((), ())), preferred_element_type=jnp.float32
    )


def live(sizes, sector):
    count = sizes.shape[0]
    inside = jnp.logical_and(sector >= 0, sector < count)
    return jnp.where(inside, sizes[jnp.clip(sector, 0, count - 1)], 0)


def charge_of(pair):
    return jnp.where(pair == 0, 0, jnp.where(pair == 3, 2, 1))


def inside(rows, cols, first_row, first_col, shape):
    row = first_row + lax.broadcasted_iota(jnp.int32, shape, 0)
    col = first_col + lax.broadcasted_iota(jnp.int32, shape, 1)
    return jnp.logical_and(row < rows, col < cols)


def gate(sizes, pair, sector):
    cols = live(sizes, sector + charge_of(pair))
    return live(sizes, sector), cols, live(sizes, sector - 1)


def kept_kernel(early, coupling, sizes, *refs):
    count = len(WIDTHS)
    own, left, right, following, upper, *rest = refs
    partner, rest = rest[:count], rest[count:]
    relayed, rest = rest[:early], rest[early:]
    acc, mixed, lower = rest
    width = mixed.shape[0]
    pair = lax.axis_index("chan")
    sector = lax.axis_index("panel")
    middle = jnp.logical_or(pair == 1, pair == 2)
    rows, cols, lower_rows = gate(sizes, pair, sector)
    alpha = coupling[0, pair, pair]
    beta = jnp.where(middle, coupling[0, pair, jnp.where(middle, 3 - pair, 0)], 0.0)

    def mix(with_partner):
        for i in range(count):
            at, wide = STARTS[i], WIDTHS[i]
            value = alpha * own[0, 0, :, at : at + wide].astype(jnp.float32)
            if with_partner:
                value = value + beta * partner[i][...].astype(jnp.float32)
            keep = inside(rows, cols, 0, at, value.shape)
            mixed[:, at : at + wide] = jnp.where(keep, value, 0.0).astype(jnp.bfloat16)

    pl.when(middle)(lambda: mix(True))
    pl.when(jnp.logical_not(middle))(lambda: mix(False))

    def kept(target):
        for at in range(0, width, TILE):
            window = pl.ds(at, TILE)
            half = jnp.dot(left[0, 0, window], mixed[...], preferred_element_type=jnp.float32)
            acc[window] = outer_dot(half.astype(jnp.bfloat16), target)

    pl.when(pair == 0)(lambda: kept(right[0, 0]))
    pl.when(pair != 0)(lambda: kept(following[...]))

    if early:
        columns = STARTS[early]
        gamma = jnp.where(pair == 0, 1.0, coupling[1, pair, 3])

        def moved(target):
            for i in range(early):
                at, wide = STARTS[i], WIDTHS[i]
                part = relayed[i][...]
                keep = inside(lower_rows, cols, 0, at, part.shape)
                lower[:, at : at + wide] = jnp.where(keep, part, jnp.zeros_like(part))
            for at in range(0, width, TILE):
                window = pl.ds(at, TILE)
                half = jnp.dot(left[1, 0, window], lower[...], preferred_element_type=jnp.float32)
                half = (gamma * half).astype(jnp.bfloat16)
                acc[window] = acc[window] + outer_dot(half, target)

        pl.when(pair == 0)(lambda: moved(right[1, 0, :, 0:columns]))
        pl.when(jnp.logical_or(pair == 1, pair == 2))(lambda: moved(upper[:, 0:columns]))


def moved_kernel(early, coupling, sizes, *refs):
    count = len(WIDTHS)
    base = STARTS[early]
    acc, left, right, upper, *rest = refs
    relayed, rest = rest[: count - early], rest[count - early :]
    out_ref, lower, out, sems = rest
    width = acc.shape[0]
    pair = lax.axis_index("chan")
    sector = lax.axis_index("panel")
    rows, cols, lower_rows = gate(sizes, pair, sector)

    def store(at, value):
        keep = inside(rows, cols, at, 0, value.shape)
        out[pl.ds(at, TILE)] = jnp.where(keep, value, 0.0).astype(jnp.bfloat16)
        send(at).start()

    def send(at):
        window = pl.ds(at, TILE)
        return pltpu.make_async_copy(out.at[window], out_ref.at[0, 0, window], sems.at[at // TILE])

    @pl.when(pair == 3)
    def _():
        for at in range(0, width, TILE):
            store(at, acc[pl.ds(at, TILE)])

    @pl.when(pair != 3)
    def _():
        for i in range(early, count):
            at, wide = STARTS[i], WIDTHS[i]
            part = relayed[i - early][...]
            keep = inside(lower_rows, cols, 0, at, part.shape)
            lower[:, at - base : at - base + wide] = jnp.where(keep, part, jnp.zeros_like(part))

    def moved(target):
        gamma = jnp.where(pair == 0, 1.0, coupling[1, pair, 3])
        for at in range(0, width, TILE):
            window = pl.ds(at, TILE)
            half = jnp.dot(left[1, 0, window], lower[...], preferred_element_type=jnp.float32)
            term = outer_dot((gamma * half).astype(jnp.bfloat16), target)
            store(at, acc[window] + term)

    pl.when(pair == 0)(lambda: moved(right[1, 0, :, base:width]))
    pl.when(jnp.logical_or(pair == 1, pair == 2))(lambda: moved(upper[:, base:width]))
    for at in range(0, width, TILE):
        send(at).wait()


def cut_kernel(blocks, count, *refs):
    sources, rest = refs[:count], refs[count:]
    targets, sems = rest[len(rest) - 1 - len(blocks) : -1], rest[-1]
    copies = []
    for i, (source, channel, at, wide) in enumerate(blocks):
        part = sources[source].at[channel, 0, :, pl.ds(at, wide)]
        copies.append(pltpu.make_async_copy(part, targets[i], sems.at[i]))
    for copy in copies:
        copy.start()
    for copy in copies:
        copy.wait()


def cut(sources, blocks, *after):
    height = sources[0].shape[-2]
    anywhere = pl.BlockSpec(memory_space=pl.ANY)
    shapes = [jax.ShapeDtypeStruct((height, wide), jnp.bfloat16) for *_, wide in blocks]
    return list(
        pl.pallas_call(
            lambda *refs: cut_kernel(blocks, len(sources), *refs),
            out_shape=shapes,
            in_specs=[anywhere] * (len(sources) + len(after)),
            out_specs=[pl.BlockSpec(memory_space=pltpu.VMEM)] * len(blocks),
            scratch_shapes=[pltpu.SemaphoreType.DMA((len(blocks),))],
            cost_estimate=pl.CostEstimate(
                flops=0, bytes_accessed=4 * height * sum(b[-1] for b in blocks), transcendentals=0
            ),
            compiler_params=pltpu.CompilerParams(vmem_limit_bytes=8 * 1024 * 1024),
        )(*sources, *after)
    )


def raise_kernel(coupling, own, partner, out):
    pair = lax.axis_index("chan")

    @pl.when(pair == 1)
    def _():
        mine = coupling[1, 0, 1] * own[...].astype(jnp.float32)
        theirs = coupling[1, 0, 2] * partner[...].astype(jnp.float32)
        out[...] = (mine + theirs).astype(jnp.bfloat16)

    @pl.when(pair == 0)
    def _():
        out[...] = partner[...]

    @pl.when(pair == 3)
    def _():
        out[...] = own[...]


def raise_part(coupling, own, partner):
    on_chip = pl.BlockSpec(memory_space=pltpu.VMEM)
    return pl.pallas_call(
        raise_kernel,
        out_shape=jax.ShapeDtypeStruct(own.shape, own.dtype),
        in_specs=[pl.BlockSpec(memory_space=pltpu.SMEM), on_chip, on_chip],
        out_specs=on_chip,
        cost_estimate=pl.CostEstimate(flops=3 * own.size, bytes_accessed=6 * own.size, transcendentals=0),
        compiler_params=pltpu.CompilerParams(vmem_limit_bytes=8 * 1024 * 1024),
        name="raise",
    )(coupling, own, partner)


def shards(wavefunction, left_env, right_env, coupling, sec_size):
    width = wavefunction.shape[-1]
    sectors = sec_size.shape[0]
    count = len(WIDTHS)
    early = count - LATE
    blocks = [(0, 0, at, wide) for at, wide in zip(STARTS, WIDTHS)]
    own_part = cut((wavefunction,), blocks[:1])
    cut_later = cut((wavefunction, right_env), blocks[1:] + [(1, 0, 0, width), (1, 1, 0, width)], own_part[0])
    own_part, right_part = own_part + cut_later[: count - 1], cut_later[count - 1 :]
    exchange = ((1, 2, 0), (2, 1, 0), (3, 0, 0))
    partner = [move(part, sectors, exchange) for part in own_part]
    nearby = ((1, 1, -1), (2, 2, -1))
    following = move(right_part[0], sectors, nearby + ((3, 3, -2),))
    upper = move(right_part[1], sectors, nearby)
    onward = ((1, 0, 1), (0, 1, 1), (3, 2, 1))
    relayed = []
    for a, b in zip(own_part, partner):
        value = raise_part(coupling, a, b)
        relayed.append(move(value, sectors, onward))

    scalars = pl.BlockSpec(memory_space=pltpu.SMEM)
    on_chip = pl.BlockSpec(memory_space=pltpu.VMEM)
    acc = pl.pallas_call(
        lambda *refs: kept_kernel(early, *refs),
        out_shape=jax.ShapeDtypeStruct((width, width), jnp.float32),
        in_specs=[scalars] * 2 + [on_chip] * (5 + count + early),
        out_specs=on_chip,
        scratch_shapes=[
            pltpu.VMEM((width, width), jnp.bfloat16),
            pltpu.VMEM((width, STARTS[early] if early else 128), jnp.bfloat16),
        ],
        cost_estimate=pl.CostEstimate(
            flops=8 * width**3, bytes_accessed=18 * width * width, transcendentals=0
        ),
        compiler_params=pltpu.CompilerParams(vmem_limit_bytes=VMEM_BYTES),
        name="kept",
    )(coupling, sec_size, wavefunction, left_env, right_env, following, upper, *partner, *relayed[:early])
    columns = width - STARTS[early]
    out = pl.pallas_call(
        lambda *refs: moved_kernel(early, *refs),
        out_shape=jax.ShapeDtypeStruct((1, 1, width, width), jnp.bfloat16),
        in_specs=[scalars] * 2 + [on_chip] * (4 + LATE),
        out_specs=pl.BlockSpec(memory_space=pl.ANY),
        scratch_shapes=[
            pltpu.VMEM((width, columns), jnp.bfloat16),
            pltpu.VMEM((width, width), jnp.bfloat16),
            pltpu.SemaphoreType.DMA((width // TILE,)),
        ],
        cost_estimate=pl.CostEstimate(
            flops=4 * width * width * columns, bytes_accessed=10 * width * width, transcendentals=0
        ),
        compiler_params=pltpu.CompilerParams(vmem_limit_bytes=VMEM_BYTES),
        name="moved",
    )(coupling, sec_size, acc, left_env, right_env, upper, *relayed[early:])
    return out


def solution(mesh):
    return jax.shard_map(
        shards,
        mesh=mesh,
        in_specs=(
            P("chan", "panel", None, None),
            P(None, "panel", None, None),
            P(None, "panel", None, None),
            P(),
            P(),
        ),
        out_specs=P("chan", "panel", None, None),
        check_vma=False,
    )
```

```python
import jax
import jax.numpy as jnp
from jax import lax
from jax.experimental import pallas as pl
from jax.experimental.pallas import tpu as pltpu
from jax.sharding import PartitionSpec as P


WIDTHS = (256, 256, 256)
STARTS = tuple(sum(WIDTHS[:i]) for i in range(len(WIDTHS)))
TILE = 256
AXES = ("panel", "chan")
VMEM_BYTES = 24 * 1024 * 1024


def move(block, sectors, routes):
    pairs = lax.axis_size("chan")
    hops = []
    for source, target, shift in routes:
        for a in range(sectors):
            if 0 <= a + shift < sectors:
                hops.append((a * pairs + source, (a + shift) * pairs + target))
    return lax.ppermute(block, AXES, hops)


def outer_dot(left_matrix, right_matrix):
    return lax.dot_general(
        left_matrix, right_matrix, (((1,), (1,)), ((), ())), preferred_element_type=jnp.float32
    )


def live(sizes, sector):
    count = sizes.shape[0]
    inside = jnp.logical_and(sector >= 0, sector < count)
    return jnp.where(inside, sizes[jnp.clip(sector, 0, count - 1)], 0)


def charge_of(pair):
    return jnp.where(pair == 0, 0, jnp.where(pair == 3, 2, 1))


def inside(rows, cols, first_row, first_col, shape):
    row = first_row + lax.broadcasted_iota(jnp.int32, shape, 0)
    col = first_col + lax.broadcasted_iota(jnp.int32, shape, 1)
    return jnp.logical_and(row < rows, col < cols)


def gate(sizes, pair, sector):
    cols = live(sizes, sector + charge_of(pair))
    return live(sizes, sector), cols, live(sizes, sector - 1)


def fill_kept(mixed, parts, scale, gates):
    rows, cols, _ = gates
    alpha, beta = scale
    base = parts[0][0]
    for at, own, other in parts:
        value = alpha * own[...].astype(jnp.float32)
        if other is not None:
            value = value + beta * other[...].astype(jnp.float32)
        keep = inside(rows, cols, 0, at, value.shape)
        mixed[:, at - base : at - base + own.shape[1]] = jnp.where(keep, value, 0.0).astype(jnp.bfloat16)


def fill_moved(lower, at, part, gates):
    _, cols, lower_rows = gates
    keep = inside(lower_rows, cols, 0, at, part.shape)
    lower[...] = jnp.where(keep, part, jnp.zeros_like(part))


def product(left, channel, at, inner, target, factor=None):
    half = jnp.dot(left[channel, 0, pl.ds(at, TILE)], inner, preferred_element_type=jnp.float32)
    if factor is not None:
        half = factor * half
    return outer_dot(half.astype(jnp.bfloat16), target)


def place(coupling, sizes):
    pair = lax.axis_index("chan")
    sector = lax.axis_index("panel")
    middle = jnp.logical_or(pair == 1, pair == 2)
    alpha = coupling[0, pair, pair]
    beta = jnp.where(middle, coupling[0, pair, jnp.where(middle, 3 - pair, 0)], 0.0)
    gamma = jnp.where(pair == 0, 1.0, coupling[1, pair, 3])
    return pair, middle, (alpha, beta), gamma, gate(sizes, pair, sector)


def kept_kernel(coupling, sizes, own0, own1, own2, left, partner0, partner1, half, mixed):
    width = half.shape[0]
    known = STARTS[2]
    _, middle, scale, _, gates = place(coupling, sizes)

    def kept(columns):
        for at in range(0, width, TILE):
            part = jnp.dot(left[0, 0, pl.ds(at, TILE)], mixed[:, 0:columns], preferred_element_type=jnp.float32)
            half[pl.ds(at, TILE), 0:columns] = part.astype(jnp.bfloat16)

    @pl.when(middle)
    def _():
        fill_kept(mixed, ((0, own0, partner0), (STARTS[1], own1, partner1)), scale, gates)
        kept(known)

    @pl.when(jnp.logical_not(middle))
    def _():
        fill_kept(mixed, [(at, own, None) for at, own in zip(STARTS, (own0, own1, own2))], scale, gates)
        kept(width)


def raised_kernel(
    coupling, sizes, own2, left, partner2, relayed0, relayed1, direct, tail, raised, mixed, lower0, lower1
):
    width = tail.shape[0]
    second, last = STARTS[1], STARTS[2]
    pair, middle, scale, gamma, gates = place(coupling, sizes)

    @pl.when(pair == 2)
    def _():
        fill_moved(lower0, 0, direct[0, 0, :, 0:second], gates)
        fill_moved(lower1, second, direct[0, 0, :, second:last], gates)

    @pl.when(pair < 2)
    def _():
        fill_moved(lower0, 0, relayed0[...], gates)
        fill_moved(lower1, second, relayed1[...], gates)

    @pl.when(middle)
    def _():
        fill_kept(mixed, ((last, own2, partner2),), scale, gates)
        for at in range(0, width, TILE):
            window = pl.ds(at, TILE)
            part = jnp.dot(left[0, 0, window], mixed[...], preferred_element_type=jnp.float32)
            tail[window] = part.astype(jnp.bfloat16)

    @pl.when(pair != 3)
    def _():
        for at in range(0, width, TILE):
            window = pl.ds(at, TILE)
            for start, wide, lower in ((0, second, lower0), (second, last - second, lower1)):
                part = jnp.dot(left[1, 0, window], lower[...], preferred_element_type=jnp.float32)
                raised[window, start : start + wide] = (gamma * part).astype(jnp.bfloat16)


def final_kernel(
    coupling, sizes, half, tail, raised, left, right, near, far, crossed, beside, direct,
    out_ref, lower, out, sems,
):
    width = out.shape[0]
    last = STARTS[2]
    pair, middle, _, gamma, gates = place(coupling, sizes)
    rows, cols, _ = gates

    def store(at, value):
        keep = inside(rows, cols, at, 0, value.shape)
        out[pl.ds(at, TILE)] = jnp.where(keep, value, 0.0).astype(jnp.bfloat16)
        send(at).start()

    def send(at):
        window = pl.ds(at, TILE)
        return pltpu.make_async_copy(out.at[window], out_ref.at[0, 0, window], sems.at[at // TILE])

    def moved(at, target):
        term = outer_dot(raised[pl.ds(at, TILE)], target[:, 0:last])
        return term + product(left, 1, at, lower[...], target[:, last:width], gamma)

    @pl.when(pair == 3)
    def _():
        for at in range(0, width, TILE):
            store(at, outer_dot(half[pl.ds(at, TILE)], far[...]))

    @pl.when(pair == 0)
    def _():
        value = coupling[1, 0, 1] * beside[...].astype(jnp.float32)
        value = value + coupling[1, 0, 2] * crossed[...].astype(jnp.float32)
        fill_moved(lower, last, value.astype(jnp.bfloat16), gates)
        for at in range(0, width, TILE):
            store(at, outer_dot(half[pl.ds(at, TILE)], right[0, 0]) + moved(at, right.at[1, 0]))

    @pl.when(middle)
    def _():
        pl.when(pair == 1)(lambda: fill_moved(lower, last, crossed[...], gates))
        pl.when(pair == 2)(lambda: fill_moved(lower, last, direct[0, 0, :, last:width], gates))
        for at in range(0, width, TILE):
            window = pl.ds(at, TILE)
            term = outer_dot(half[window, 0:last], near[0, 0, :, 0:last])
            term = term + outer_dot(tail[window], near[0, 0, :, last:width])
            store(at, term + moved(at, near.at[1, 0]))

    for at in range(0, width, TILE):
        send(at).wait()


def cut_kernel(blocks, count, *refs):
    sources, rest = refs[:count], refs[count:]
    targets, sems = rest[len(rest) - 1 - len(blocks) : -1], rest[-1]
    copies = []
    for i, (source, channel, at, wide) in enumerate(blocks):
        part = sources[source].at[channel, 0, :, pl.ds(at, wide)]
        copies.append(pltpu.make_async_copy(part, targets[i], sems.at[i]))
    for copy in copies:
        copy.start()
    for copy in copies:
        copy.wait()


def cut(sources, blocks, *after):
    height = sources[0].shape[-2]
    anywhere = pl.BlockSpec(memory_space=pltpu.HBM)
    shapes = [jax.ShapeDtypeStruct((height, wide), jnp.bfloat16) for *_, wide in blocks]
    return list(
        pl.pallas_call(
            lambda *refs: cut_kernel(blocks, len(sources), *refs),
            out_shape=shapes,
            in_specs=[anywhere] * (len(sources) + len(after)),
            out_specs=[pl.BlockSpec(memory_space=pltpu.VMEM)] * len(blocks),
            scratch_shapes=[pltpu.SemaphoreType.DMA((len(blocks),))],
            cost_estimate=pl.CostEstimate(
                flops=0, bytes_accessed=4 * height * sum(b[-1] for b in blocks), transcendentals=0
            ),
            compiler_params=pltpu.CompilerParams(vmem_limit_bytes=8 * 1024 * 1024),
        )(*sources, *after)
    )


def raise_kernel(coupling, own, partner, out):
    pair = lax.axis_index("chan")

    @pl.when(pair == 1)
    def _():
        mine = coupling[1, 0, 1] * own[...].astype(jnp.float32)
        theirs = coupling[1, 0, 2] * partner[...].astype(jnp.float32)
        out[...] = (mine + theirs).astype(jnp.bfloat16)

    @pl.when(pair == 0)
    def _():
        out[...] = partner[...]


def raise_part(coupling, own, partner):
    on_chip = pl.BlockSpec(memory_space=pltpu.VMEM)
    return pl.pallas_call(
        raise_kernel,
        out_shape=jax.ShapeDtypeStruct(own.shape, own.dtype),
        in_specs=[pl.BlockSpec(memory_space=pltpu.SMEM), on_chip, on_chip],
        out_specs=on_chip,
        cost_estimate=pl.CostEstimate(flops=3 * own.size, bytes_accessed=6 * own.size, transcendentals=0),
        compiler_params=pltpu.CompilerParams(vmem_limit_bytes=8 * 1024 * 1024),
        name="raise",
    )(coupling, own, partner)


def shards(wavefunction, left_env, right_env, coupling, sec_size):
    width = wavefunction.shape[-1]
    sectors = sec_size.shape[0]
    blocks = [(0, 0, at, wide) for at, wide in zip(STARTS, WIDTHS)]
    (first,) = cut((wavefunction,), blocks[:1])
    second, third = cut((wavefunction,), blocks[1:], first)
    (right_low,) = cut((right_env,), [(0, 0, 0, width)], third)
    swap = ((1, 2, 0), (2, 1, 0))
    own_part = (first, second)
    partner = [move(part, sectors, swap + ((3, 0, 0),)) for part in own_part]
    partner_last = move(third, sectors, swap)
    crossed = move(third, sectors, ((2, 0, 1), (3, 1, 1)))
    beside = move(third, sectors, ((1, 0, 1),))
    direct = move(wavefunction, sectors, ((3, 2, 1),))
    near = move(right_env, sectors, ((1, 1, -1), (2, 2, -1)))
    far = move(right_low, sectors, ((3, 3, -2),))
    onward = ((1, 0, 1), (0, 1, 1))
    relayed = []
    for a, b in zip(own_part, partner):
        value = raise_part(coupling, a, b)
        relayed.append(move(value, sectors, onward))

    scalars = pl.BlockSpec(memory_space=pltpu.SMEM)
    on_chip = pl.BlockSpec(memory_space=pltpu.VMEM)

    def call(kernel, flops, out_shape, out_spec, scratch, *args):
        cost = pl.CostEstimate(flops=flops, bytes_accessed=12 * width * width, transcendentals=0)
        return pl.pallas_call(
            kernel,
            out_shape=out_shape,
            in_specs=[scalars] * 2 + [on_chip] * len(args),
            out_specs=out_spec,
            scratch_shapes=scratch,
            cost_estimate=cost,
            compiler_params=pltpu.CompilerParams(vmem_limit_bytes=VMEM_BYTES),
        )(coupling, sec_size, *args)

    part = pltpu.VMEM((width, TILE), jnp.bfloat16)
    block = pltpu.VMEM((width, width), jnp.bfloat16)
    half = call(
        kept_kernel, 2 * width**3, jax.ShapeDtypeStruct((width, width), jnp.bfloat16), on_chip, [block],
        first, second, third, left_env, *partner,
    )
    sides = [jax.ShapeDtypeStruct((width, wide), jnp.bfloat16) for wide in (width - STARTS[2], STARTS[2])]
    tail, raised = call(
        raised_kernel, 2 * width**3, sides, [on_chip] * 2, [part] * 3,
        third, left_env, partner_last, *relayed, direct,
    )
    return call(
        final_kernel, 5 * width**3,
        jax.ShapeDtypeStruct((1, 1, width, width), jnp.bfloat16), pl.BlockSpec(memory_space=pl.ANY),
        [part, block, pltpu.SemaphoreType.DMA((width // TILE,))],
        half, tail, raised, left_env, right_env, near, far, crossed, beside, direct,
    )


def solution(mesh):
    return jax.shard_map(
        shards,
        mesh=mesh,
        in_specs=(
            P("chan", "panel", None, None),
            P(None, "panel", None, None),
            P(None, "panel", None, None),
            P(),
            P(),
        ),
        out_specs=P("chan", "panel", None, None),
        check_vma=False,
    )
```
